32 devices in a mesh: row: 4 (over y, core), col: 8 (over z, x).
Axes of the slice: x: 2, y: 2, z: 4, core: 2. Of those that a mesh axis runs over, the one named last changes fastest.
Arguments:
- orbitals: bfloat16 [4, 8, 1024, 512], P('row', 'col'), may hold values from -6 to 6
- tiles: bfloat16 [4, 8, 60, 128, 128], P('row', 'col'), may hold values from -0.1875 to 0.1875
- tile_rows: int32 [4, 8, 60], P('row', 'col'), may hold values from 0 to 7, as said below
- tile_cols: int32 [4, 8, 60], P('row', 'col'), may hold values from 0 to 13
Outputs:
- product: bfloat16 [4, 8, 1024, 512], P('row', 'col')
The draws below stay inside these ranges and needn't reach their ends.
Inputs may be any that keep to these rules, and one draw needn't show every extreme that they name: The pairs (tile_rows, tile_cols) of one grid position are distinct, and tile_rows <= tile_cols wherever tile_cols < 8.
All inputs are finite; a program needn't handle non-finite values.
Results may differ from the reference program's by a relative error of at most 0.001.
Values may be sent and summed in bfloat16 or wider, within the bound.
No kernel may reach another device: no remote copies, remote signals or barrier semaphores. Data moves between devices by JAX's collectives and lax.ppermute only.
A program may use at most 64 MiB of HBM per device.

```python
import jax
import jax.numpy as jnp
import numpy as np
from jax import lax

BS = 128
OCC = 512
CB = 8
RIM = 2
NCAND = 84
TILE_DEV = 60
N_ROW = 4
N_COL = 8


def tile_pairs(key):
    anchor_list = []
    target_list = []
    for upper in range(CB):
        for lower in range(upper, CB):
            anchor_list.append(upper)
            target_list.append(lower)
    for upper in range(CB):
        for remote in range(3 * RIM):
            anchor_list.append(upper)
            target_list.append(CB + remote)
    anchor_table = jnp.asarray(np.array(anchor_list, dtype=np.int32))
    target_table = jnp.asarray(np.array(target_list, dtype=np.int32))
    keys = jax.random.split(jax.random.fold_in(key, 11), N_ROW * N_COL)
    picks = jax.vmap(lambda single: jax.random.permutation(single, NCAND)[:TILE_DEV])(keys)
    anchors = anchor_table[picks].reshape(N_ROW, N_COL, TILE_DEV).astype(jnp.int32)
    targets = target_table[picks].reshape(N_ROW, N_COL, TILE_DEV).astype(jnp.int32)
    return (anchors, targets)


def draw_tile_rows(key, part):
    return tile_pairs(key)[0]


def draw_tile_cols(key, part):
    return tile_pairs(key)[1]


def level_of(stream_key, extent, shards, least, top_value):
    level, own = 1.0, jax.random.fold_in(stream_key, 6)
    for position, blocks in shards:
        heights = jnp.exp(jax.random.uniform(jax.random.fold_in(own, position), (blocks,), jnp.float32, least / len(shards), top_value / len(shards)))
        level = level * jnp.repeat(heights, extent[position] // blocks).reshape([-1 if axis == position else 1 for axis in range(len(extent))])
    return level


def centred(rng, shape, spread, most, pieces=(), kind=jnp.bfloat16):
    values = spread * jax.random.normal(rng, shape, jnp.float32)
    if pieces:
        values = values * level_of(rng, shape, pieces, -0.22, 0.18)
    return jnp.clip(values, -most, most).astype(kind)


def setup_inputs(seed: int = 0) -> dict:
    seeds = jax.random.split(jax.random.key(seed), 5)
    orbitals = centred(seeds[0], (N_ROW, N_COL, CB * BS, OCC), 1.0, 6.0, ((0, 4), (1, 8)))
    tiles = centred(seeds[1], (N_ROW, N_COL, TILE_DEV, BS, BS), (BS * 8) ** -0.5, 0.1875, ((0, 4), (1, 8)))
    tile_rows = draw_tile_rows(jax.random.fold_in(seeds[4], 71), 0)
    tile_cols = draw_tile_cols(jax.random.fold_in(seeds[4], 71), 0)
    return {"orbitals": orbitals, "tiles": tiles, "tile_rows": tile_rows, "tile_cols": tile_cols}


def device_terms(tiles_here, anchors, targets, extended):
    fetched = extended[targets].astype(jnp.float32)
    sources = extended[anchors].astype(jnp.float32)
    blocks = tiles_here.astype(jnp.float32)
    forward = jnp.einsum('tab,tbn->tan', blocks, fetched)
    keep = (anchors != targets).astype(jnp.float32)
    mirrored = jnp.einsum('tab,tan->tbn', blocks, sources) * keep[:, None, None]
    partial_value = jnp.zeros((CB + 3 * RIM, BS, OCC), jnp.float32)
    partial_value = partial_value.at[anchors].add(forward)
    partial_value = partial_value.at[targets].add(mirrored)
    return partial_value


def reference(orbitals, tiles, tile_rows, tile_cols):
    grouped = orbitals.reshape(N_ROW, N_COL, CB, BS, OCC)

    def one_position(flat):
        row_pos = flat // N_COL
        col_pos = flat % N_COL
        next_row = (row_pos + 1) % N_ROW
        next_col = (col_pos + 1) % N_COL
        extended = jnp.concatenate([
            grouped[row_pos, col_pos],
            grouped[row_pos, next_col, :RIM],
            grouped[next_row, col_pos, :RIM],
            grouped[next_row, next_col, :RIM]], axis=0)
        partial_value = device_terms(tiles[row_pos, col_pos], tile_rows[row_pos, col_pos],
                               tile_cols[row_pos, col_pos], extended)
        return partial_value[:CB], partial_value[CB:]

    owned, rims = lax.map(one_position, jnp.arange(N_ROW * N_COL, dtype=jnp.int32))
    owned = owned.reshape(N_ROW, N_COL, CB, BS, OCC)
    rims = rims.reshape(N_ROW, N_COL, 3 * RIM, BS, OCC)
    to_col = rims[:, :, :RIM]
    to_row = rims[:, :, RIM:2 * RIM]
    to_diag = rims[:, :, 2 * RIM:]
    incoming = jnp.roll(to_col, 1, axis=1) + jnp.roll(to_row, 1, axis=0)
    incoming = incoming + jnp.roll(jnp.roll(to_diag, 1, axis=0), 1, axis=1)
    owned = owned.at[:, :, :RIM].add(incoming)
    return owned.reshape(N_ROW, N_COL, CB * BS, OCC).astype(jnp.bfloat16)
```

```python
import jax
import jax.numpy as jnp
from jax import lax
from jax.experimental import pallas as pl
from jax.experimental.pallas import tpu as pltpu
from jax.sharding import PartitionSpec as P

BS = 128
CB = 8
RIM = 2


VMEM = pl.BlockSpec(memory_space=pltpu.VMEM)
SMEM = pl.BlockSpec(memory_space=pltpu.SMEM)


def shifted(shard, axis, by):
    size = lax.axis_size(axis)
    return lax.ppermute(shard, axis, [(i, (i + by) % size) for i in range(size)])


def mirror_kernel(rows, cols, tiles, owned, remote, to_col, to_row, to_diag, dense):
    n_tiles = tiles.shape[0]
    width = 3 * RIM * BS
    dense[...] = jnp.zeros_like(dense)
    for t in range(n_tiles):
        row, col = rows[0, 0, t], cols[0, 0, t]
        slot = jnp.where(col >= CB, col - CB, 3 * RIM)
        dense[pl.ds(pl.multiple_of(row * BS, BS), BS), pl.ds(pl.multiple_of(slot * BS, BS), BS)] = tiles[t]
    for k, out in ((2, to_diag), (1, to_row), (0, to_col)):
        part = dense[:, k * RIM * BS:(k + 1) * RIM * BS]
        remote[k] = part
        out[...] = lax.dot_general(part, owned[...], (((0,), (0,)), ((), ())), preferred_element_type=jnp.float32)


def own_kernel(rows, cols, tiles, owned, total, dense):
    n_tiles = tiles.shape[0]
    dense[...] = jnp.zeros_like(dense)
    for t in range(n_tiles):
        row, col = rows[0, 0, t], cols[0, 0, t]
        slot = jnp.where(col < CB, col, CB)
        dense[pl.ds(pl.multiple_of(row * BS, BS), BS), pl.ds(pl.multiple_of(slot * BS, BS), BS)] = tiles[t]
    for i in range(CB):
        for j in range(i + 1, CB):
            dense[j * BS:(j + 1) * BS, i * BS:(i + 1) * BS] = dense[i * BS:(i + 1) * BS, j * BS:(j + 1) * BS].T
    total[...] = jnp.dot(dense[:, :CB * BS], owned[...], preferred_element_type=jnp.float32)


def finish_kernel(total, remote, beside, below, corner, from_row, from_col, out):
    acc = total[...]
    for k, rim in enumerate((beside, below, corner)):
        acc += jnp.dot(remote[k], rim[...], preferred_element_type=jnp.float32)
    out[RIM * BS:, :] = acc[RIM * BS:].astype(out.dtype)
    out[:RIM * BS, :] = (acc[:RIM * BS] + from_row[...] + from_col[...]).astype(out.dtype)


def body(orbitals, tiles, tile_rows, tile_cols):
    occ = orbitals.shape[-1]
    rim_rows = RIM * BS
    owned = orbitals.reshape(CB * BS, occ)
    stored = tiles.reshape(-1, BS, BS)
    rim = owned[:rim_rows]
    beside = shifted(rim, "col", -1)
    below = shifted(rim, "row", -1)
    f32 = jnp.float32
    part = jax.ShapeDtypeStruct((rim_rows, occ), f32)
    remote, to_col, to_row, to_diag = pl.pallas_call(
        mirror_kernel,
        out_shape=(jax.ShapeDtypeStruct((3, CB * BS, rim_rows), jnp.bfloat16), part, part, part),
        in_specs=[SMEM, SMEM, VMEM, VMEM],
        out_specs=(VMEM,) * 4,
        scratch_shapes=[pltpu.VMEM((CB * BS, (3 * RIM + 1) * BS), jnp.bfloat16)],
        name="mirror",
    )(tile_rows, tile_cols, stored, owned)
    from_diag = shifted(to_diag, "row", 1)
    from_row = shifted(to_row, "row", 1)
    corner = shifted(beside, "row", -1)
    from_col = shifted(to_col + from_diag, "col", 1)
    total = pl.pallas_call(
        own_kernel,
        out_shape=jax.ShapeDtypeStruct((CB * BS, occ), f32),
        in_specs=[SMEM, SMEM, VMEM, VMEM],
        out_specs=VMEM,
        scratch_shapes=[pltpu.VMEM((CB * BS, (CB + 1) * BS), jnp.bfloat16)],
        name="own",
    )(tile_rows, tile_cols, stored, owned)
    out = pl.pallas_call(
        finish_kernel,
        out_shape=jax.ShapeDtypeStruct((CB * BS, occ), jnp.bfloat16),
        in_specs=[VMEM] * 7,
        out_specs=VMEM,
        name="finish",
    )(total, remote, beside, below, corner, from_row, from_col)
    return out.reshape(orbitals.shape)


def solution(mesh):
    return jax.shard_map(
        body,
        mesh=mesh,
        in_specs=(
            P("row", "col", None, None),
            P("row", "col", None, None, None),
            P("row", "col", None),
            P("row", "col", None),
        ),
        out_specs=P("row", "col", None, None),
        check_vma=False,
    )
```

```python
import jax
import jax.numpy as jnp
from jax import lax
from jax.experimental import pallas as pl
from jax.experimental.pallas import tpu as pltpu
from jax.sharding import PartitionSpec as P


BS = 128
CB = 8
RIM = 2
SCALE = 16.0


VMEM = pl.BlockSpec(memory_space=pltpu.VMEM)
ANY = pl.BlockSpec(memory_space=pl.ANY)
F32, BF16 = jnp.float32, jnp.bfloat16


def shifted(shard, axis, by):
    size = lax.axis_size(axis)
    return lax.ppermute(shard, axis, [(i, (i + by) % size) for i in range(size)])


def here(x):
    return pltpu.with_memory_space_constraint(x, pltpu.VMEM)


def there(x):
    return pltpu.with_memory_space_constraint(x, pltpu.HBM)


def call(kernel, out_shape, operands, in_specs=None, **options):
    many = isinstance(out_shape, tuple)
    if in_specs is None:
        in_specs = [VMEM] * len(operands)
        operands = [here(x) for x in operands]
    return pl.pallas_call(
        kernel,
        out_shape=out_shape,
        in_specs=in_specs,
        compiler_params=pltpu.CompilerParams(vmem_limit_bytes=24 << 20),
        **{"out_specs": (VMEM,) * len(out_shape) if many else VMEM, **options},
    )(*operands)


def dot(a, b):
    return jnp.dot(a, b, preferred_element_type=F32)


def transposed_dot(a, b):
    return lax.dot_general(a, b, (((0,), (0,)), ((), ())), preferred_element_type=F32)


def rim_columns(k):
    first = (CB + k * RIM) * BS
    return slice(first, first + RIM * BS)


def gather_kernel(rows_hbm, cols_hbm, tiles_hbm, owned_hbm, dense, owned, rim, to_diag, tiles, rows, cols, sems):
    copies = [
        pltpu.make_async_copy(rows_hbm, rows, sems.at[0]),
        pltpu.make_async_copy(cols_hbm, cols, sems.at[1]),
        pltpu.make_async_copy(tiles_hbm, tiles, sems.at[2]),
        pltpu.make_async_copy(owned_hbm, owned, sems.at[3]),
    ]
    for copy in copies:
        copy.start()
    dense[...] = jnp.zeros_like(dense)
    for copy in copies[:3]:
        copy.wait()
    for t in range(tiles.shape[0]):
        row, col = rows[0, 0, t], cols[0, 0, t]
        dense[pl.ds(pl.multiple_of(row * BS, BS), BS), pl.ds(pl.multiple_of(col * BS, BS), BS)] = tiles[t]
    copies[3].wait()
    rim[...] = owned[:RIM * BS, :]
    to_diag[...] = transposed_dot(dense[:, rim_columns(2)], owned[...])


def mirror_kernel(dense, owned, to_col, to_row):
    to_row[...] = transposed_dot(dense[:, rim_columns(1)], owned[...])
    to_col[...] = transposed_dot(dense[:, rim_columns(0)], owned[...])


def own_kernel(dense, owned, total, square):
    for i in range(CB):
        block = slice(i * BS, (i + 1) * BS)
        square[block, i * BS:CB * BS] = dense[block, i * BS:CB * BS]
        for j in range(i + 1, CB):
            square[j * BS:(j + 1) * BS, block] = dense[block, j * BS:(j + 1) * BS].T
    total[...] = dot(square[...], owned[...])


def beside_kernel(total, dense, beside, below, more):
    more[...] = total[...] + dot(dense[:, rim_columns(0)], beside[...]) + dot(dense[:, rim_columns(1)], below[...])


def finish_kernel(total, dense, corner, from_row, from_col, out):
    acc = total[...] + dot(dense[:, rim_columns(2)], corner[...])
    out[RIM * BS:, :] = acc[RIM * BS:].astype(out.dtype)
    out[:RIM * BS, :] = (acc[:RIM * BS] + from_row[...] + from_col[...]).astype(out.dtype)


def inner_body(orbitals, tiles, tile_rows, tile_cols):
    occ = orbitals.shape[-1]
    rim_rows = RIM * BS
    owned_hbm = orbitals.reshape(CB * BS, occ)
    stored = tiles.reshape(-1, BS, BS)
    part = pltpu.VMEM((rim_rows, occ), F32)
    whole = pltpu.VMEM((CB * BS, occ), F32)
    dense, owned, rim, to_diag = call(
        gather_kernel,
        (pltpu.VMEM((CB * BS, (CB + 3 * RIM) * BS), BF16), pltpu.VMEM((CB * BS, occ), BF16), pltpu.VMEM((rim_rows, occ), BF16), part),
        [there(x) for x in (tile_rows, tile_cols, stored, owned_hbm)],
        in_specs=[ANY] * 4,
        scratch_shapes=[
            pltpu.VMEM(stored.shape, BF16),
            pltpu.SMEM(tile_rows.shape, jnp.int32),
            pltpu.SMEM(tile_cols.shape, jnp.int32),
            pltpu.SemaphoreType.DMA((4,)),
        ],
    )
    to_col, to_row = call(mirror_kernel, (part, part), (dense, owned))
    enc = lambda x: (x * SCALE).astype(jnp.float16)
    dec = lambda x: x.astype(F32) * (1 / SCALE)
    from_diag = shifted(enc(to_diag), "row", 1)
    beside = shifted(rim, "col", -1)
    from_row = shifted(enc(to_row), "row", 1)
    below = shifted(rim, "row", -1)
    corner = shifted(beside, "row", -1)
    from_col = shifted(enc(to_col + dec(from_diag)), "col", 1)
    total = call(own_kernel, whole, (dense, owned), scratch_shapes=[pltpu.VMEM((CB * BS, CB * BS), BF16)])
    total = call(beside_kernel, whole, (total, dense, beside, below))
    out = call(finish_kernel, jax.ShapeDtypeStruct((CB * BS, occ), BF16), (total, dense, corner, dec(from_row), dec(from_col)))
    return out.reshape(orbitals.shape)


def solution(mesh):
    return jax.shard_map(
        inner_body,
        mesh=mesh,
        in_specs=(
            P("row", "col", None, None),
            P("row", "col", None, None, None),
            P("row", "col", None),
            P("row", "col", None),
        ),
        out_specs=P("row", "col", None, None),
        check_vma=False,
    )
```

```python
import jax
import jax.numpy as jnp
from jax import lax
from jax.experimental import pallas as pl
from jax.experimental.pallas import tpu as pltpu
from jax.sharding import PartitionSpec as P


BS = 128
CB = 8
RIM = 2
SCALE = 16.0
PIECES = 2


VMEM = pl.BlockSpec(memory_space=pltpu.VMEM)
ANY = pl.BlockSpec(memory_space=pl.ANY)
F32, BF16 = jnp.float32, jnp.bfloat16


def shifted(shard, axis, by):
    size = lax.axis_size(axis)
    return lax.ppermute(shard, axis, [(i, (i + by) % size) for i in range(size)])


def here(x):
    return pltpu.with_memory_space_constraint(x, pltpu.VMEM)


def there(x):
    return pltpu.with_memory_space_constraint(x, pltpu.HBM)


def call(kernel, out_shape, operands, in_specs=None, **options):
    many = isinstance(out_shape, tuple)
    if in_specs is None:
        in_specs = [VMEM] * len(operands)
        operands = [here(x) for x in operands]
    return pl.pallas_call(
        kernel,
        out_shape=out_shape,
        in_specs=in_specs,
        compiler_params=pltpu.CompilerParams(vmem_limit_bytes=24 << 20),
        **{"out_specs": (VMEM,) * len(out_shape) if many else VMEM, **options},
    )(*operands)


def dot(a, b):
    return jnp.dot(a, b, preferred_element_type=F32)


def transposed_dot(a, b):
    return lax.dot_general(a, b, (((0,), (0,)), ((), ())), preferred_element_type=F32)


def rim_columns(k):
    first = (CB + k * RIM) * BS
    return slice(first, first + RIM * BS)


def gather_kernel(rows_hbm, cols_hbm, tiles_hbm, owned_hbm, dense, owned, rim, to_diag, tiles, rows, cols, sems):
    n_tiles = tiles.shape[0]
    bounds = [n_tiles * k // PIECES for k in range(PIECES + 1)]
    index = [pltpu.make_async_copy(rows_hbm, rows, sems.at[0]), pltpu.make_async_copy(cols_hbm, cols, sems.at[1])]
    pieces = [
        pltpu.make_async_copy(tiles_hbm.at[pl.ds(lo, hi - lo)], tiles.at[pl.ds(lo, hi - lo)], sems.at[3 + k])
        for k, (lo, hi) in enumerate(zip(bounds, bounds[1:]))
    ]
    mine = pltpu.make_async_copy(owned_hbm, owned, sems.at[2])
    for copy in index + pieces + [mine]:
        copy.start()
    dense[...] = jnp.zeros_like(dense)
    for copy in index:
        copy.wait()
    for k, copy in enumerate(pieces):
        copy.wait()
        for t in range(bounds[k], bounds[k + 1]):
            row, col = rows[0, 0, t], cols[0, 0, t]
            dense[pl.ds(pl.multiple_of(row * BS, BS), BS), pl.ds(pl.multiple_of(col * BS, BS), BS)] = tiles[t]
    mine.wait()
    to_diag[...] = transposed_dot(dense[:, rim_columns(2)], owned[...])
    rim[...] = owned[:RIM * BS, :]


def early_kernel(dense, owned, to_col, to_row):
    @pl.when(lax.axis_index("col") == 0)
    def _():
        to_row[...] = transposed_dot(dense[:, rim_columns(1)], owned[...])
        to_col[...] = transposed_dot(dense[:, rim_columns(0)], owned[...])


def late_kernel(dense, owned, early_col, early_row, to_col, to_row):
    del early_col, early_row

    @pl.when(lax.axis_index("col") != 0)
    def _():
        to_row[...] = transposed_dot(dense[:, rim_columns(1)], owned[...])
        to_col[...] = transposed_dot(dense[:, rim_columns(0)], owned[...])


def own_kernel(dense, owned, total, square):
    for i in range(CB):
        block = slice(i * BS, (i + 1) * BS)
        square[block, i * BS:CB * BS] = dense[block, i * BS:CB * BS]
        for j in range(i + 1, CB):
            square[j * BS:(j + 1) * BS, block] = dense[block, j * BS:(j + 1) * BS].T
    total[...] = dot(square[...], owned[...])


def beside_kernel(total, dense, beside, below, more):
    more[...] = total[...] + dot(dense[:, rim_columns(0)], beside[...]) + dot(dense[:, rim_columns(1)], below[...])


def bulk_kernel(total, dense, corner, from_row, lead, out, rest, sems):
    rim_rows = RIM * BS
    corner_columns = rim_columns(2)
    copies = []
    for k in range(1, CB // RIM):
        rows = pl.ds(k * rim_rows, rim_rows)
        here_rows = pl.ds((k - 1) * rim_rows, rim_rows)
        rest[here_rows, :] = (total[rows, :] + dot(dense[rows, corner_columns], corner[...])).astype(rest.dtype)
        copies.append(pltpu.make_async_copy(rest.at[here_rows], out.at[rows], sems.at[k - 1]))
        copies[-1].start()
    lead[...] = total[:rim_rows, :] + dot(dense[:rim_rows, corner_columns], corner[...]) + from_row[...]
    for copy in copies:
        copy.wait()


def inner_body(orbitals, tiles, tile_rows, tile_cols):
    occ = orbitals.shape[-1]
    rim_rows = RIM * BS
    owned_hbm = orbitals.reshape(CB * BS, occ)
    stored = tiles.reshape(-1, BS, BS)
    part = pltpu.VMEM((rim_rows, occ), F32)
    whole = pltpu.VMEM((CB * BS, occ), F32)
    dense, owned, rim, to_diag = call(
        gather_kernel,
        (pltpu.VMEM((CB * BS, (CB + 3 * RIM) * BS), BF16), pltpu.VMEM((CB * BS, occ), BF16), pltpu.VMEM((rim_rows, occ), BF16), part),
        [there(x) for x in (tile_rows, tile_cols, stored, owned_hbm)],
        in_specs=[ANY] * 4,
        scratch_shapes=[
            pltpu.VMEM(stored.shape, BF16),
            pltpu.SMEM(tile_rows.shape, jnp.int32),
            pltpu.SMEM(tile_cols.shape, jnp.int32),
            pltpu.SemaphoreType.DMA((3 + PIECES,)),
        ],
    )
    early = call(early_kernel, (part, part), (dense, owned))
    to_col, to_row = call(late_kernel, (part, part), (dense, owned, *early), input_output_aliases={2: 0, 3: 1})
    enc = lambda x: (x * SCALE).astype(jnp.float16)
    dec = lambda x: x.astype(F32) * (1 / SCALE)
    from_diag = shifted(enc(to_diag), "row", 1)
    beside = shifted(rim, "col", -1)
    from_row = shifted(enc(to_row), "row", 1)
    below = shifted(rim, "row", -1)
    corner = shifted(beside, "row", -1)
    from_col = shifted(enc(to_col + dec(from_diag)), "col", 1)
    total = call(own_kernel, whole, (dense, owned), scratch_shapes=[pltpu.VMEM((CB * BS, CB * BS), BF16)])
    total = call(beside_kernel, whole, (total, dense, beside, below))
    lead, out = call(
        bulk_kernel, (part, pltpu.HBM((CB * BS, occ), BF16)), (total, dense, corner, dec(from_row)),
        out_specs=(VMEM, ANY),
        scratch_shapes=[pltpu.VMEM(((CB - RIM) * BS, occ), BF16), pltpu.SemaphoreType.DMA((CB // RIM - 1,))],
    )
    out = lax.dynamic_update_slice(out, (lead + dec(from_col)).astype(BF16), (0, 0))
    return out.reshape(orbitals.shape)


def solution(mesh):
    return jax.shard_map(
        inner_body,
        mesh=mesh,
        in_specs=(
            P("row", "col", None, None),
            P("row", "col", None, None, None),
            P("row", "col", None),
            P("row", "col", None),
        ),
        out_specs=P("row", "col", None, None),
        check_vma=False,
    )
```
